256 devices in a mesh: ctx: 8 (over z), exp: 32 (over y, x, core).
Axes of the slice: x: 4, y: 4, z: 8, core: 2. Of those that a mesh axis runs over, the one named last changes fastest.
Arguments:
- query_rows: bfloat16 [6144, 4096], P('ctx', 'exp'), may hold values from -6 to 6
- key_rows: bfloat16 [6144, 4096], P('ctx', 'exp'), may hold values from -6 to 6
- value_rows: bfloat16 [6144, 4096], P('ctx', 'exp'), may hold values from -6 to 6
- log_decay: float32 [32, 6144], P('exp', 'ctx'), may hold values from -1 to 0
- residual: bfloat16 [6144, 3072], P(('ctx', 'exp')), may hold values from -20 to 20
- norm_gain: float32 [3072], replicated, may hold values from 0.1 to 1.9
- out_grad: bfloat16 [6144, 3072], P(('ctx', 'exp')), may hold values from -6 to 6
- experts_of: int32 [6144, 2], P(('ctx', 'exp')), may hold values from 0 to 31, all different within a row; in each aligned block of 24 rows (0 to 23, 24 to 47, ...) at most 2 rows name the same one
- route_weight: float32 [6144, 2], P(('ctx', 'exp')), may hold values from 0.1 to 0.9
- output_weight: bfloat16 [4096, 3072], P('exp'), may hold values from -0.09375 to 0.09375
- expert_gate: bfloat16 [32, 3072, 4608], P('exp', None, 'ctx'), may hold values from -0.109375 to 0.109375
- expert_up: bfloat16 [32, 3072, 4608], P('exp', None, 'ctx'), may hold values from -0.109375 to 0.109375
- expert_down: bfloat16 [32, 4608, 3072], P('exp', 'ctx'), may hold values from -0.09375 to 0.09375
Outputs:
- query_grad: bfloat16 [6144, 4096], P('ctx', 'exp')
- key_grad: bfloat16 [6144, 4096], P('ctx', 'exp')
- value_grad: bfloat16 [6144, 4096], P('ctx', 'exp')
The draws below stay inside these ranges and needn't reach their ends.
Inputs may be any that keep to these rules, and one draw needn't show every extreme that they name: `experts_of`: in each aligned block of 24 tokens (the tokens of one device) no expert is named by more than 2 tokens, a bound that some block reaches; a token's two experts differ.
All inputs are finite; a program needn't handle non-finite values.
Results may differ from the reference program's by a relative error of at most 0.017.
Values may be sent and summed in bfloat16 or wider, within the bound.
No kernel may reach another device: no remote copies, remote signals or barrier semaphores. Data moves between devices by JAX's collectives and lax.ppermute only.
A program may use at most 128 MiB of HBM per device.

```python
import math
from functools import partial
import jax
import jax.numpy as jnp
import numpy as np
from jax import lax

D = 3072
F = 4608
HD = 128
TOK_DEV = 24
HEAD_COUNT = 32
EXPERTS = 32
D_ATTN = 4096
F_PART = 576
CAP = 2
BLOCK = 768
WINDOW_TOKENS = 6144
N_CTX = 8
N_EXP = 32


def draw_log_decay(key, part):
    random_subkeys = jax.random.split(key, 6)
    share = 0.5
    rapid_head = jax.random.uniform(random_subkeys[0], (HEAD_COUNT, 1), jnp.float32) < share
    rapid_decay_rate = jnp.exp(jax.random.uniform(random_subkeys[1], (HEAD_COUNT, 1), jnp.float32, math.log(1.0 / 50.0), math.log(1.0 / 30.0)))
    gentle_decay_rate = jnp.exp(jax.random.uniform(random_subkeys[2], (HEAD_COUNT, 1), jnp.float32, math.log(0.05 / WINDOW_TOKENS), math.log(0.6 / WINDOW_TOKENS)))
    random_offset = jax.random.uniform(random_subkeys[3], (HEAD_COUNT, WINDOW_TOKENS), jnp.float32, 0.5, 1.5)
    spike_position = jax.random.randint(random_subkeys[4], (HEAD_COUNT, 2), 0, WINDOW_TOKENS)
    token_position = jnp.arange(WINDOW_TOKENS, dtype=jnp.int32)[None, :]
    spike_flag = (token_position == spike_position[:, 0:1]) | (token_position == spike_position[:, 1:2])
    spike_penalty = jax.random.uniform(random_subkeys[5], (HEAD_COUNT, WINDOW_TOKENS), jnp.float32, math.log(1.25), math.log(2.0))
    per_step_rate = jnp.where(rapid_head, rapid_decay_rate, gentle_decay_rate) * random_offset + jnp.where(spike_flag, spike_penalty, 0.0)
    return (-per_step_rate).astype(jnp.float32)


def draw_residual(key, part):
    random_subkeys = jax.random.split(key, 3)
    base_draw = jnp.clip(jax.random.normal(random_subkeys[0], (WINDOW_TOKENS, D), jnp.float32), -4.0, 4.0)
    row_scale = jnp.exp(jax.random.uniform(random_subkeys[1], (WINDOW_TOKENS, 1), jnp.float32, math.log(0.05), math.log(0.5)))
    col_scale = jnp.exp(jax.random.uniform(random_subkeys[2], (1, D), jnp.float32, 0.0, math.log(10.0)))
    return (base_draw * row_scale * col_scale).astype(jnp.bfloat16)


def shard_levels(stream_key, shape, shards, least, largest):
    factor_of, own = 1.0, jax.random.fold_in(stream_key, 6)
    for axis_at, parts in shards:
        heights = jnp.exp(jax.random.uniform(jax.random.fold_in(own, axis_at), (parts,), jnp.float32, least / len(shards), largest / len(shards)))
        factor_of = factor_of * jnp.repeat(heights, shape[axis_at] // parts).reshape([-1 if axis == axis_at else 1 for axis in range(len(shape))])
    return factor_of


def deal_out(rng, own, number, rows, count, top, limit, skew):
    ranking = jax.random.permutation(rng, count)
    crowded, usual = load_shares(count, rows * top, limit, skew, True), load_shares(count, rows * top, limit, skew, False)
    places = jnp.arange(count)

    def named(sizes, offset_by):
        used = int((sizes > 0).sum())
        fixed = max(1, used // 4)
        moved = fixed + (places - fixed + offset_by * (used - fixed)) % max(1, count - fixed)
        return jnp.zeros((count,), jnp.int32).at[ranking[jnp.where(places < fixed, places, moved)]].set(jnp.asarray(sizes, jnp.int32))

    sizes = jnp.where(number % 4 == 0, named(crowded, number // 4), named(usual, number - number // 4 - 1))
    mixed = jax.random.permutation(jax.random.fold_in(own, 3), count)
    donor, sink = mixed[0:count // 2 * 2:2], mixed[1:count // 2 * 2:2]
    slack = jnp.minimum(sizes[donor] - 1, limit - sizes[sink]) // 2
    slack = jnp.where((donor == ranking[0]) | (sink == ranking[0]) | (sizes[sink] == 0), 0, jnp.maximum(slack, 0))
    moved = jax.random.randint(jax.random.fold_in(own, 4), (count // 2,), 0, 1 << 20) % (slack + 1)
    sizes = sizes.at[donor].add(-moved).at[sink].add(moved)
    labels = jnp.searchsorted(jnp.cumsum(sizes), jnp.arange(rows * top), side="right").astype(jnp.int32)
    listing = labels.reshape(top, rows).T
    listing = listing[jax.random.permutation(jax.random.fold_in(own, 1), rows)]
    offset_by = jax.random.randint(jax.random.fold_in(own, 2), (rows, 1), 0, top)
    return jnp.take_along_axis(listing, (jnp.arange(top)[None, :] + offset_by) % top, axis=1)


def load_shares(amount, total, bound, skew, full):
    portions = [(1 << 20) // math.isqrt(rank ** skew) + 1 for rank in range(1, amount + 1)]
    largest = bound if full else min(bound, max(-(-total // amount), total * portions[0] // sum(portions)))
    least = 1 if total - largest >= amount - 1 else 0
    holding, spare = [largest] + [least] * (amount - 1), total - largest - least * (amount - 1)
    while spare > 0:
        movable = [i for i in range(1, amount) if holding[i] < largest] or [i for i in range(1, amount) if holding[i] < bound]
        whole, budget = sum([portions[i] for i in movable]), spare
        for i in movable:
            more = min(bound - holding[i], max(1, budget * portions[i] // whole), spare)
            holding[i] = holding[i] + more
            spare = spare - more
    return np.array(holding)


def normal_values(stream_key, dims, scale, reach, shards=(), kind=jnp.bfloat16):
    loudness = shard_levels(stream_key, dims, shards, -0.22, 0.18) if shards else 1.0
    entries = jax.random.normal(stream_key, dims, jnp.float32) * scale * loudness
    return jnp.minimum(jnp.maximum(entries, -reach), reach).astype(kind)


def setup_inputs(seed: int = 0) -> dict:
    splits = jax.random.split(jax.random.key(seed), 14)
    query_rows = normal_values(splits[0], (WINDOW_TOKENS, D_ATTN), 1.0, 6.0, ((0, 8), (1, 32)))
    key_rows = normal_values(splits[1], (WINDOW_TOKENS, D_ATTN), 1.0, 6.0, ((0, 8), (1, 32)))
    value_rows = normal_values(splits[2], (WINDOW_TOKENS, D_ATTN), 1.0, 6.0, ((0, 8), (1, 32)))
    log_decay = draw_log_decay(jax.random.fold_in(splits[13], 71), 0)
    residual = draw_residual(jax.random.fold_in(splits[13], 71), 0)
    norm_gain = jnp.clip(1.0 + 0.18 * jax.random.normal(splits[5], (D,), jnp.float32), 0.1, 1.9)
    out_grad = normal_values(splits[6], (WINDOW_TOKENS, D), 1.0, 6.0, ((0, 256),))
    experts_of_keys = jax.random.split(jax.random.fold_in(splits[7], 1), WINDOW_TOKENS // TOK_DEV)
    experts_of_turns = jax.random.permutation(jax.random.fold_in(splits[7], 3), WINDOW_TOKENS // TOK_DEV)
    experts_of = jax.vmap(lambda own, number: deal_out(jax.random.fold_in(splits[7], 2), own, number, TOK_DEV, EXPERTS, 2, CAP, 2))(experts_of_keys, experts_of_turns).reshape((WINDOW_TOKENS, 2))
    route_weight = jnp.clip(0.1 + 0.79999997 * jax.random.uniform(splits[8], (WINDOW_TOKENS, 2), jnp.float32) ** shard_levels(splits[8], (WINDOW_TOKENS, 2), ((0, 256),), -0.2, 0.2), 0.1, 0.9)
    output_weight = normal_values(splits[9], (D_ATTN, D), D_ATTN ** -0.5, 0.09375, ((0, 32),))
    expert_gate = normal_values(splits[10], (EXPERTS, D, F), D ** -0.5, 0.109375, ((0, 32), (2, 8)))
    expert_up = normal_values(splits[11], (EXPERTS, D, F), D ** -0.5, 0.109375, ((0, 32), (2, 8)))
    expert_down = normal_values(splits[12], (EXPERTS, F, D), F ** -0.5, 0.09375, ((0, 32), (1, 8)))
    return dict(query_rows=query_rows, key_rows=key_rows, value_rows=value_rows, log_decay=log_decay, residual=residual, norm_gain=norm_gain, out_grad=out_grad, experts_of=experts_of, route_weight=route_weight, output_weight=output_weight, expert_gate=expert_gate, expert_up=expert_up, expert_down=expert_down)


def normalize(residual, norm_gain):
    residual_f = residual.astype(jnp.float32)
    factor = lax.rsqrt(lax.optimization_barrier(jnp.mean(residual_f * residual_f, axis=-1, keepdims=True)) + 1e-05)
    return (residual_f, factor, (residual_f * factor * norm_gain).astype(jnp.bfloat16))

def slot_table(experts_of, count, capacity):
    flat_ids = experts_of.reshape(-1)
    matches = (flat_ids[:, None] == jnp.arange(count, dtype=jnp.int32)[None, :]).astype(jnp.int32)
    before = jnp.cumsum(matches, axis=0, dtype=jnp.int32) - matches
    target = flat_ids * capacity + lax.optimization_barrier(jnp.sum(before * matches, axis=1, dtype=jnp.int32))
    slots = jnp.arange(count * capacity, dtype=jnp.int32)
    return (slots[:, None] == target[None, :]).astype(jnp.bfloat16)

def pack_rows(expert_input, out_grad, route_weight, slot_onehot, count, capacity):
    routed = (route_weight[:, :, None] * out_grad.astype(jnp.float32)[:, None, :]).astype(jnp.bfloat16)
    inputs = jnp.broadcast_to(expert_input[:, None, :], routed.shape)
    packed = jnp.concatenate([inputs, routed], axis=-1).reshape(slot_onehot.shape[1], -1)
    outgoing = jnp.dot(slot_onehot, packed, preferred_element_type=jnp.float32).astype(jnp.bfloat16)
    return outgoing.reshape(count, capacity, packed.shape[1])

def expert_rows(row_block, gate_mat, up_mat, down_mat):
    features = gate_mat.shape[0]
    row_input = row_block[:, :features]
    row_grad = row_block[:, features:]
    gate_pre = jnp.dot(row_input, gate_mat, preferred_element_type=jnp.float32)
    up_pre = jnp.dot(row_input, up_mat, preferred_element_type=jnp.float32)
    hidden_grad = lax.dot_general(row_grad, down_mat, (((1,), (1,)), ((), ())), preferred_element_type=jnp.float32)
    gate_sig = jax.nn.sigmoid(gate_pre)
    gate_grad = (hidden_grad * up_pre * gate_sig * (1.0 + gate_pre * (1.0 - gate_sig))).astype(jnp.bfloat16)
    up_grad = (hidden_grad * gate_pre * gate_sig).astype(jnp.bfloat16)
    first = lax.dot_general(gate_grad, gate_mat, (((1,), (1,)), ((), ())), preferred_element_type=jnp.float32)
    second = lax.dot_general(up_grad, up_mat, (((1,), (1,)), ((), ())), preferred_element_type=jnp.float32)
    return first + second

def resid_backward(residual_f, factor, out_grad, slot_onehot, returned, norm_gain):
    per_row = lax.dot_general(slot_onehot, returned.reshape(slot_onehot.shape[0], -1), (((0,), (0,)), ((), ())), preferred_element_type=jnp.float32)
    moe_grad = lax.optimization_barrier(jnp.sum(per_row.reshape(-1, 2, per_row.shape[1]), axis=1))
    scaled = norm_gain * moe_grad
    unit_rows = residual_f * factor
    total_grad = out_grad.astype(jnp.float32) + factor * (scaled - unit_rows * lax.optimization_barrier(jnp.mean(unit_rows * scaled, axis=-1, keepdims=True)))
    return total_grad.astype(jnp.bfloat16)

def block_terms(query_part, key_part, value_part, grad_part, log_steps, score_scale):
    levels = jnp.cumsum(log_steps)
    block_total = levels[-1]
    from_start = jnp.exp(levels)
    to_end = jnp.exp(block_total - levels)
    key_state = lax.dot_general(key_part.astype(jnp.float32) * to_end[:, None], value_part.astype(jnp.float32), (((0,), (0,)), ((), ())), precision=lax.Precision.HIGHEST)
    adjoint = score_scale * lax.dot_general(query_part.astype(jnp.float32) * from_start[:, None], grad_part.astype(jnp.float32), (((0,), (0,)), ((), ())), precision=lax.Precision.HIGHEST)
    return (levels, jnp.exp(block_total), key_state, adjoint)

def block_grads(query_part, key_part, value_part, grad_part, levels, state_in, adjoint_out, score_scale):
    block_total = levels[-1]
    from_start = jnp.exp(levels)
    to_end = jnp.exp(block_total - levels)
    token_position = jnp.arange(levels.shape[0], dtype=jnp.int32)
    causal = token_position[:, None] >= token_position[None, :]
    fading = jnp.exp(jnp.where(causal, levels[:, None] - levels[None, :], -jnp.inf))
    scores = lax.dot_general(query_part, key_part, (((1,), (1,)), ((), ())), preferred_element_type=jnp.float32)
    attn_probs = (score_scale * scores * fading).astype(jnp.bfloat16)
    grad_scores = lax.dot_general(grad_part, value_part, (((1,), (1,)), ((), ())), preferred_element_type=jnp.float32)
    pull_weights = (score_scale * grad_scores * fading).astype(jnp.bfloat16)
    grad_f = grad_part.astype(jnp.float32)
    query_out = jnp.dot(pull_weights, key_part, preferred_element_type=jnp.float32)
    query_out = query_out + score_scale * from_start[:, None] * lax.dot_general(grad_f, state_in, (((1,), (1,)), ((), ())), precision=lax.Precision.HIGHEST)
    key_out = lax.dot_general(pull_weights, query_part, (((0,), (0,)), ((), ())), preferred_element_type=jnp.float32)
    key_out = key_out + to_end[:, None] * lax.dot_general(value_part.astype(jnp.float32), adjoint_out, (((1,), (1,)), ((), ())), precision=lax.Precision.HIGHEST)
    value_out = lax.dot_general(attn_probs, grad_part, (((0,), (0,)), ((), ())), preferred_element_type=jnp.float32)
    value_out = value_out + to_end[:, None] * jnp.dot(key_part.astype(jnp.float32), adjoint_out, precision=lax.Precision.HIGHEST)
    return (query_out.astype(jnp.bfloat16), key_out.astype(jnp.bfloat16), value_out.astype(jnp.bfloat16))

def reference(query_rows, key_rows, value_rows, log_decay, residual, norm_gain, out_grad, experts_of, route_weight, output_weight, expert_gate, expert_up, expert_down):
    blocks = N_CTX * N_EXP
    resid_blocks = residual.reshape(blocks, TOK_DEV, D)
    grad_blocks = out_grad.reshape(blocks, TOK_DEV, D)
    route_blocks = experts_of.reshape(blocks, TOK_DEV, 2)
    weight_blocks = route_weight.reshape(blocks, TOK_DEV, 2)
    residual_f, factor, expert_input = jax.vmap(partial(normalize, norm_gain=norm_gain))(resid_blocks)
    dispatches = jax.vmap(partial(slot_table, count=EXPERTS, capacity=CAP))(route_blocks)
    outgoing = jax.vmap(partial(pack_rows, count=EXPERTS, capacity=CAP))(expert_input, grad_blocks, weight_blocks, dispatches)
    by_expert = jnp.transpose(outgoing, (1, 0, 2, 3)).reshape(EXPERTS, blocks * CAP, 2 * D)

    def expert_block(operands):
        row_block, gate_mat, up_mat, down_mat = operands
        summed_rows = jnp.zeros((row_block.shape[0], D), jnp.float32)
        for group_index in range(N_CTX):
            start_unit = group_index * F_PART
            end_unit = start_unit + F_PART
            group_term = expert_rows(row_block, gate_mat[:, start_unit:end_unit], up_mat[:, start_unit:end_unit], down_mat[start_unit:end_unit]).astype(jnp.bfloat16)
            summed_rows = summed_rows + lax.optimization_barrier(group_term).astype(jnp.float32)
        return summed_rows.astype(jnp.bfloat16)
    finished = lax.map(expert_block, (by_expert, expert_gate, expert_up, expert_down))
    returned = jnp.transpose(finished.reshape(EXPERTS, blocks, CAP, D), (1, 0, 2, 3))
    resid_grad = jax.vmap(partial(resid_backward, norm_gain=norm_gain))(residual_f, factor, grad_blocks, dispatches, returned)
    resid_grad = resid_grad.reshape(WINDOW_TOKENS, D)
    attn_grad = lax.dot_general(resid_grad, output_weight, (((1,), (1,)), ((), ())), preferred_element_type=jnp.float32).astype(jnp.bfloat16)
    score_scale = 1.0 / math.sqrt(HD * WINDOW_TOKENS)

    def by_head(array):
        return jnp.transpose(array.reshape(N_CTX, BLOCK, HEAD_COUNT, HD), (2, 0, 1, 3))
    steps_all = log_decay.reshape(HEAD_COUNT, N_CTX, BLOCK)

    def head_backward(operands):
        query_part, key_part, value_part, grad_part, log_steps = operands
        levels, block_gain, key_state, adjoint = jax.vmap(partial(block_terms, score_scale=score_scale))(query_part, key_part, value_part, grad_part, log_steps)
        zero_state = jnp.zeros((HD, HD), jnp.float32)

        def forward_step(carry, element):
            gain_now, state_now = element
            return (gain_now * carry + state_now, carry)
        _, state_in = lax.scan(forward_step, zero_state, (block_gain, key_state))

        def backward_step(carry, element):
            gain_now, adjoint_now = element
            return (adjoint_now + gain_now * carry, carry)
        _, adjoint_out = lax.scan(backward_step, zero_state, (block_gain, adjoint), reverse=True)
        return jax.vmap(partial(block_grads, score_scale=score_scale))(query_part, key_part, value_part, grad_part, levels, state_in, adjoint_out)
    results = lax.map(head_backward, (by_head(query_rows), by_head(key_rows), by_head(value_rows), by_head(attn_grad), steps_all))

    def merge_heads(array):
        return jnp.transpose(array, (1, 2, 0, 3)).reshape(WINDOW_TOKENS, D_ATTN)
    return (merge_heads(results[0]), merge_heads(results[1]), merge_heads(results[2]))
```

```python
import math
from functools import partial

import jax
import jax.numpy as jnp
from jax import lax
from jax.experimental import pallas as pl
from jax.experimental.pallas import tpu as pltpu
from jax.sharding import PartitionSpec as P


BF = jnp.bfloat16
F32 = jnp.float32
Y_COUNT = 4
X_COUNT = 4
GROUP = 8
EXPERTS = 32


def nt(a, b):
    return lax.dot_general(a, b, (((1,), (1,)), ((), ())), preferred_element_type=F32)


def nn(a, b):
    return lax.dot_general(a, b, (((1,), (0,)), ((), ())), preferred_element_type=F32)


def tn(a, b):
    return lax.dot_general(a, b, (((0,), (0,)), ((), ())), preferred_element_type=F32)


def whole(shape):
    return pl.BlockSpec(shape, lambda *_: (0,) * len(shape))


def as_column(row):
    count = row.shape[1]
    eye = lax.broadcasted_iota(jnp.int32, (count, count), 0) == lax.broadcasted_iota(
        jnp.int32, (count, count), 1
    )
    return jnp.sum(jnp.where(eye, jnp.broadcast_to(row, (count, count)), 0.0), axis=1, keepdims=True)


def slot_places(experts, count):
    tokens = experts.shape[1]
    ids = lax.broadcasted_iota(jnp.int32, (count, tokens), 0)
    first = jnp.where(ids == experts[0:1, :], 1.0, 0.0)
    second = jnp.where(ids == experts[1:2, :], 1.0, 0.0)
    before = jnp.where(
        lax.broadcasted_iota(jnp.int32, (tokens, tokens), 0)
        < lax.broadcasted_iota(jnp.int32, (tokens, tokens), 1),
        1.0,
        0.0,
    )
    taken0 = nn(first.astype(BF), before.astype(BF))
    taken1 = nn(second.astype(BF), before.astype(BF)) + jnp.sum(first, axis=1, keepdims=True)
    place0 = jnp.sum(taken0 * first, axis=0, keepdims=True) + 2.0 * experts[0:1, :].astype(F32)
    place1 = jnp.sum(taken1 * second, axis=0, keepdims=True) + 2.0 * experts[1:2, :].astype(F32)
    return place0, place1


def unit_scale(residual_f):
    return lax.rsqrt(jnp.mean(residual_f * residual_f, axis=-1, keepdims=True) + 1e-05)


def pack_kernel(residual_ref, gain_ref, grad_ref, experts_ref, weight_ref, out_ref):
    tokens, features = residual_ref.shape
    lanes = out_ref.shape[1]
    pieces = features // lanes
    residual_f = residual_ref[...].astype(F32)
    rows = residual_f * unit_scale(residual_f) * gain_ref[...]
    grad_f = grad_ref[...].astype(F32)
    weights = weight_ref[...]
    routed0 = as_column(weights[0:1, :]) * grad_f
    routed1 = as_column(weights[1:2, :]) * grad_f
    place0, place1 = slot_places(experts_ref[...], EXPERTS)

    def piece(array, i):
        return array[:, i * lanes : (i + 1) * lanes]

    stack = [piece(rows, i) for i in range(pieces)]
    for i in range(pieces):
        stack = stack + [piece(routed0, i), piece(routed1, i)]
    stack = jnp.concatenate(stack, 0).astype(BF)
    depth = stack.shape[0]
    spread_row = lax.broadcasted_iota(jnp.int32, (tokens, depth), 1)
    spread = jnp.where(
        spread_row - ((spread_row * 2731) >> 16) * 24
        == lax.broadcasted_iota(jnp.int32, (tokens, depth), 0),
        1.0,
        0.0,
    ).astype(BF)
    at0 = nn(place0.astype(BF), spread).astype(jnp.int32)
    at1 = nn(place1.astype(BF), spread).astype(jnp.int32)
    shape = (out_ref.shape[0], depth)
    row = lax.broadcasted_iota(jnp.int32, shape, 0)
    block = (lax.broadcasted_iota(jnp.int32, (1, depth), 1) * 2731) >> 16
    over = block - pieces
    index = jnp.where(block < pieces, block, pieces + (over >> 1))
    use0 = (block < pieces) | ((over & 1) == 0)
    use1 = (block < pieces) | ((over & 1) == 1)
    at0 = jnp.where(use0, at0 * 8 + index, -1)
    at1 = jnp.where(use1, at1 * 8 + index, -1)
    chosen = jnp.where(row == at0, 1.0, 0.0) + jnp.where(row == at1, 1.0, 0.0)
    out_ref[...] = nn(chosen.astype(BF), stack).astype(BF)


def unpack_kernel(rows_ref, going_ref, coming_ref):
    lanes = rows_ref.shape[1]
    half = going_ref.shape[0]
    shape = (half, 8 * half)
    for side, out_ref in enumerate((going_ref, coming_ref)):
        block = rows_ref[side * 8 * half : (side + 1) * 8 * half, :]
        for i in range(8):
            pick = jnp.where(
                lax.broadcasted_iota(jnp.int32, shape, 1)
                == lax.broadcasted_iota(jnp.int32, shape, 0) * 8 + i,
                1.0,
                0.0,
            ).astype(BF)
            out_ref[:, i * lanes : (i + 1) * lanes] = nn(pick, block).astype(BF)


def expert_kernel(*refs, first):
    if first:
        going, coming, gate, up, down, out_f, out_b, rows, acc = refs
    else:
        going, coming, recv_f, recv_b, gate, up, down, out_f, out_b, rows, acc = refs
    half = going.shape[0]
    features = gate.shape[1]
    step = pl.program_id(0)

    @pl.when(step == 0)
    def _():
        rows[:half, :] = going[...]
        rows[half:, :] = coming[...]
        if first:
            acc[...] = jnp.zeros_like(acc)
        else:
            acc[:half, :] = recv_f[...].astype(F32)
            acc[half:, :] = recv_b[...].astype(F32)

    row_input = rows[:, :features]
    row_grad = rows[:, features:]
    gate_mat = gate[...]
    up_mat = up[...]
    gate_pre = nt(row_input, gate_mat)
    up_pre = nt(row_input, up_mat)
    hidden_grad = nt(row_grad, down[...])
    gate_sig = 1.0 / (1.0 + jnp.exp(-gate_pre))
    gate_grad = (hidden_grad * up_pre * gate_sig * (1.0 + gate_pre * (1.0 - gate_sig))).astype(BF)
    up_grad = (hidden_grad * gate_pre * gate_sig).astype(BF)
    acc[...] += nn(gate_grad, gate_mat) + nn(up_grad, up_mat)

    @pl.when(step == pl.num_programs(0) - 1)
    def _():
        out_f[...] = acc[:half, :].astype(out_f.dtype)
        out_b[...] = acc[half:, :].astype(out_b.dtype)


def expert_step(going, coming, gate, up, down, received=None, keep=BF):
    half, width = going.shape
    hidden, features = gate.shape
    block = hidden // 3
    extra = () if received is None else received
    spec = pl.BlockSpec((block, features), lambda i: (i, 0))
    return pl.pallas_call(
        partial(expert_kernel, first=received is None),
        grid=(3,),
        in_specs=[whole((half, width))] * 2 + [whole((half, features))] * len(extra) + [spec] * 3,
        out_specs=[whole((half, features))] * 2,
        out_shape=[jax.ShapeDtypeStruct((half, features), keep)] * 2,
        scratch_shapes=[pltpu.VMEM((2 * half, width), BF), pltpu.VMEM((2 * half, features), F32)],
        compiler_params=pltpu.CompilerParams(vmem_limit_bytes=40 << 20),
        name="expert_step" if extra else "expert_own",
    )(going, coming, *extra, gate, up, down)


def finish_kernel(own_f, own_b, recv_f, recv_b, out_ref):
    lanes = out_ref.shape[1]
    sums = jnp.concatenate(
        [own_f[...] + recv_f[...].astype(F32), own_b[...] + recv_b[...].astype(F32)], 0
    )
    count, features = sums.shape
    pieces = features // lanes
    stack = jnp.concatenate(
        [sums[:, i * lanes : (i + 1) * lanes] for i in range(pieces)], 0
    ).astype(BF)
    shape = (count * pieces, count * pieces)
    row = lax.broadcasted_iota(jnp.int32, shape, 0)
    column = lax.broadcasted_iota(jnp.int32, shape, 1)
    pick = jnp.where(column == (row & (pieces - 1)) * count + (row >> 2), 1.0, 0.0).astype(BF)
    out_ref[...] = nn(pick, stack).astype(BF)


def resid_kernel(returned_ref, residual_ref, gain_ref, grad_ref, experts_ref, out_ref):
    tokens, features = residual_ref.shape
    lanes = returned_ref.shape[1]
    pieces = features // lanes
    place0, place1 = slot_places(experts_ref[...], EXPERTS)
    at0 = as_column(place0).astype(jnp.int32) * pieces
    at1 = as_column(place1).astype(jnp.int32) * pieces
    returned = returned_ref[...]
    shape = (tokens, returned.shape[0])
    column = lax.broadcasted_iota(jnp.int32, shape, 1)
    moe = []
    for i in range(pieces):
        pick = jnp.where(column == at0 + i, 1.0, 0.0) + jnp.where(column == at1 + i, 1.0, 0.0)
        moe.append(nn(pick.astype(BF), returned))
    scaled = gain_ref[...] * jnp.concatenate(moe, 1)
    residual_f = residual_ref[...].astype(F32)
    factor = unit_scale(residual_f)
    unit_rows = residual_f * factor
    inner = jnp.mean(unit_rows * scaled, axis=-1, keepdims=True)
    total = grad_ref[...].astype(F32) + factor * (scaled - unit_rows * inner)
    out_ref[...] = total.astype(BF)


def single(kernel, shapes, *operands):
    return pl.pallas_call(
        kernel,
        out_shape=[jax.ShapeDtypeStruct(shape, BF) for shape in shapes],
        compiler_params=pltpu.CompilerParams(vmem_limit_bytes=40 << 20),
    )(*operands)


def body(
    query_rows,
    key_rows,
    value_rows,
    log_decay,
    residual,
    norm_gain,
    out_grad,
    experts_of,
    route_weight,
    output_weight,
    expert_gate,
    expert_up,
    expert_down,
):
    ctx_count = lax.axis_size("ctx")
    exp_count = lax.axis_size("exp")
    token_count, features = residual.shape
    block_len, head_size = query_rows.shape
    score_scale = 1.0 / math.sqrt(head_size * block_len * ctx_count)
    forward = [(i, (i + 1) % ctx_count) for i in range(ctx_count)]
    backward = [(i, (i - 1) % ctx_count) for i in range(ctx_count)]

    gain_row = norm_gain.reshape(1, features)
    experts = jnp.swapaxes(experts_of, 0, 1)
    (outgoing,) = single(
        pack_kernel,
        [(exp_count * 16, features // 4)],
        residual,
        gain_row,
        out_grad,
        experts,
        jnp.swapaxes(route_weight, 0, 1),
    )
    arrived = lax.all_to_all(outgoing, "exp", split_axis=0, concat_axis=0, tiled=True)

    place = lax.axis_index("exp")
    core = place % 2
    x_at = (place // 2) % X_COUNT
    partner = lax.ppermute(output_weight, "exp", [(i, i ^ 1) for i in range(exp_count)])
    head_rows = output_weight.shape[0]
    pair = jnp.where(
        core == 0,
        jnp.concatenate([output_weight, partner], 0),
        jnp.concatenate([partner, output_weight], 0),
    )
    near = jnp.zeros((X_COUNT, 2 * head_rows, features), BF)
    for shift in range(X_COUNT):
        moved = pair
        if shift:
            link = [
                (i, (i // 8) * 8 + ((i // 2 - shift) % X_COUNT) * 2 + i % 2) for i in range(exp_count)
            ]
            moved = lax.ppermute(pair, "exp", link)
        near = lax.dynamic_update_index_in_dim(near, moved, (x_at + shift) % X_COUNT, 0)
    near = near.reshape(GROUP * head_rows, features)

    levels = jnp.cumsum(log_decay[0])
    block_total = levels[-1]
    from_start = jnp.exp(levels)
    to_end = jnp.exp(block_total - levels)
    key_state = tn((key_rows.astype(F32) * to_end[:, None]).astype(BF), value_rows)
    gate_t = jnp.swapaxes(expert_gate[0], 0, 1)
    up_t = jnp.swapaxes(expert_up[0], 0, 1)
    down = expert_down[0]
    going, coming = single(unpack_kernel, [(exp_count, 2 * features)] * 2, arrived)
    sums = None
    for step in range(ctx_count):
        if step < ctx_count - 1:
            next_going = lax.ppermute(going, "ctx", forward)
            next_coming = lax.ppermute(coming, "ctx", backward)
        if step == 0:
            own = expert_step(going, coming, gate_t, up_t, down, None, F32)
        else:
            sums = expert_step(going, coming, gate_t, up_t, down, sums)
        if step:
            sum_f = lax.ppermute(sums[0], "ctx", forward)
            sum_b = lax.ppermute(sums[1], "ctx", backward)
            sums = (sum_f, sum_b)
        going, coming = next_going, next_coming
    (summed,) = single(finish_kernel, [(exp_count * 8, features // 4)], *own, *sums)

    returned = lax.all_to_all(summed, "exp", split_axis=0, concat_axis=0, tiled=True)
    (resid_grad,) = single(
        resid_kernel, [(token_count, features)], returned, residual, gain_row, out_grad, experts
    )

    columns = [[j * GROUP + i for j in range(Y_COUNT)] for i in range(GROUP)]
    lines = [[j * GROUP + i for i in range(GROUP)] for j in range(Y_COUNT)]
    gathered = lax.all_gather(resid_grad, "exp", axis=0, tiled=True, axis_index_groups=columns)
    attn_part = nt(gathered, near).astype(BF)
    attn_grad = lax.all_to_all(
        attn_part, "exp", split_axis=1, concat_axis=0, tiled=True, axis_index_groups=lines
    )
    attn_grad = attn_grad.reshape(GROUP, Y_COUNT, token_count, head_size)
    attn_grad = jnp.transpose(attn_grad, (1, 0, 2, 3)).reshape(block_len, head_size)

    adjoint = score_scale * tn((query_rows.astype(F32) * from_start[:, None]).astype(BF), attn_grad)
    here = lax.axis_index("ctx")
    order8 = jnp.arange(ctx_count, dtype=jnp.int32)
    outward = jnp.where((order8 > here)[:, None, None], key_state[None], adjoint[None]).astype(BF)
    top = lax.reduce_precision(block_total, 8, 7)
    middle = lax.reduce_precision(block_total - top, 8, 7)
    bottom = block_total - top - middle
    line = jnp.stack([top, middle, bottom] + [jnp.zeros((), F32)] * 5).astype(BF)
    line = jnp.broadcast_to(line[None, :, None], (ctx_count, 8, head_size))
    outward = jnp.concatenate([outward, line], 1)
    inward = lax.all_to_all(outward, "ctx", split_axis=0, concat_axis=0, tiled=True)
    totals = jnp.sum(inward[:, head_size : head_size + 3, 0].astype(F32), axis=1)
    between = (order8[None, :] > jnp.minimum(order8, here)[:, None]) & (
        order8[None, :] < jnp.maximum(order8, here)[:, None]
    )
    reach = jnp.exp(jnp.sum(jnp.where(between, totals[None, :], 0.0), axis=1))
    blocks = inward[:, :head_size, :].astype(F32)
    state_in = jnp.sum(jnp.where(order8 < here, reach, 0.0)[:, None, None] * blocks, axis=0)
    adjoint_out = jnp.sum(jnp.where(order8 > here, reach, 0.0)[:, None, None] * blocks, axis=0)

    order = jnp.arange(block_len, dtype=jnp.int32)
    causal = order[:, None] >= order[None, :]
    fading = jnp.exp(jnp.where(causal, levels[:, None] - levels[None, :], -jnp.inf))
    probs = (score_scale * nt(query_rows, key_rows) * fading).astype(BF)
    pull = (score_scale * nt(attn_grad, value_rows) * fading).astype(BF)
    query_out = nn(pull, key_rows) + score_scale * from_start[:, None] * nt(attn_grad, state_in.astype(BF))
    adjoint_bf = adjoint_out.astype(BF)
    key_out = tn(pull, query_rows) + to_end[:, None] * nt(value_rows, adjoint_bf)
    value_out = tn(probs, attn_grad) + to_end[:, None] * nn(key_rows, adjoint_bf)
    return query_out.astype(BF), key_out.astype(BF), value_out.astype(BF)


def solution(mesh):
    placed = (
        P("ctx", "exp"),
        P("ctx", "exp"),
        P("ctx", "exp"),
        P("exp", "ctx"),
        P(("ctx", "exp"), None),
        P(),
        P(("ctx", "exp"), None),
        P(("ctx", "exp"), None),
        P(("ctx", "exp"), None),
        P("exp", None),
        P("exp", None, "ctx"),
        P("exp", None, "ctx"),
        P("exp", "ctx", None),
    )
    return jax.shard_map(
        body,
        mesh=mesh,
        in_specs=placed,
        out_specs=(P("ctx", "exp"), P("ctx", "exp"), P("ctx", "exp")),
        check_vma=False,
    )
```

```python
import math

import jax
import jax.numpy as jnp
from jax import lax
from jax.experimental import pallas as pl
from jax.experimental.pallas import tpu as pltpu
from jax.sharding import PartitionSpec as P


BF = jnp.bfloat16
F32 = jnp.float32
Y_COUNT = 4
X_COUNT = 4
GROUP = 8
EXPERTS = 32
WIDE = 52 << 20


def nt(a, b):
    return lax.dot_general(a, b, (((1,), (1,)), ((), ())), preferred_element_type=F32)


def nn(a, b):
    return lax.dot_general(a, b, (((1,), (0,)), ((), ())), preferred_element_type=F32)


def tn(a, b):
    return lax.dot_general(a, b, (((0,), (0,)), ((), ())), preferred_element_type=F32)


def whole(shape):
    return pl.BlockSpec(shape, lambda *_: (0,) * len(shape))


def as_column(row):
    count = row.shape[1]
    eye = lax.broadcasted_iota(jnp.int32, (count, count), 0) == lax.broadcasted_iota(
        jnp.int32, (count, count), 1
    )
    return jnp.sum(jnp.where(eye, jnp.broadcast_to(row, (count, count)), 0.0), axis=1, keepdims=True)


def slot_places(experts, count):
    tokens = experts.shape[1]
    ids = lax.broadcasted_iota(jnp.int32, (count, tokens), 0)
    first = jnp.where(ids == experts[0:1, :], 1.0, 0.0)
    second = jnp.where(ids == experts[1:2, :], 1.0, 0.0)
    before = jnp.where(
        lax.broadcasted_iota(jnp.int32, (tokens, tokens), 0)
        < lax.broadcasted_iota(jnp.int32, (tokens, tokens), 1),
        1.0,
        0.0,
    )
    taken0 = nn(first.astype(BF), before.astype(BF))
    taken1 = nn(second.astype(BF), before.astype(BF)) + jnp.sum(first, axis=1, keepdims=True)
    place0 = jnp.sum(taken0 * first, axis=0, keepdims=True) + 2.0 * experts[0:1, :].astype(F32)
    place1 = jnp.sum(taken1 * second, axis=0, keepdims=True) + 2.0 * experts[1:2, :].astype(F32)
    return place0, place1


def unit_scale(residual_f):
    return lax.rsqrt(jnp.mean(residual_f * residual_f, axis=-1, keepdims=True) + 1e-05)


def pack_kernel(residual_ref, gain_ref, grad_ref, experts_ref, weight_ref, out_ref):
    tokens, features = residual_ref.shape
    lanes = out_ref.shape[1]
    pieces = features // lanes
    residual_f = residual_ref[...].astype(F32)
    rows = residual_f * unit_scale(residual_f) * gain_ref[...]
    grad_f = grad_ref[...].astype(F32)
    weights = weight_ref[...]
    routed0 = as_column(weights[0:1, :]) * grad_f
    routed1 = as_column(weights[1:2, :]) * grad_f
    place0, place1 = slot_places(experts_ref[...], EXPERTS)

    def piece(array, i):
        return array[:, i * lanes : (i + 1) * lanes]

    stack = [piece(rows, i) for i in range(pieces)]
    for i in range(pieces):
        stack = stack + [piece(routed0, i), piece(routed1, i)]
    stack = jnp.concatenate(stack, 0).astype(BF)
    depth = stack.shape[0]
    spread_row = lax.broadcasted_iota(jnp.int32, (tokens, depth), 1)
    spread = jnp.where(
        spread_row - ((spread_row * 2731) >> 16) * 24
        == lax.broadcasted_iota(jnp.int32, (tokens, depth), 0),
        1.0,
        0.0,
    ).astype(BF)
    at0 = nn(place0.astype(BF), spread).astype(jnp.int32)
    at1 = nn(place1.astype(BF), spread).astype(jnp.int32)
    shape = (out_ref.shape[0], depth)
    row = lax.broadcasted_iota(jnp.int32, shape, 0)
    block = (lax.broadcasted_iota(jnp.int32, (1, depth), 1) * 2731) >> 16
    over = block - pieces
    index = jnp.where(block < pieces, block, pieces + (over >> 1))
    use0 = (block < pieces) | ((over & 1) == 0)
    use1 = (block < pieces) | ((over & 1) == 1)
    at0 = jnp.where(use0, at0 * 8 + index, -1)
    at1 = jnp.where(use1, at1 * 8 + index, -1)
    chosen = jnp.where(row == at0, 1.0, 0.0) + jnp.where(row == at1, 1.0, 0.0)
    out_ref[...] = nn(chosen.astype(BF), stack).astype(BF)


def unpack_kernel(rows_ref, going_ref, coming_ref):
    lanes = rows_ref.shape[1]
    half = going_ref.shape[0]
    shape = (half, 8 * half)
    for side, out_ref in enumerate((going_ref, coming_ref)):
        block = rows_ref[side * 8 * half : (side + 1) * 8 * half, :]
        for i in range(8):
            pick = jnp.where(
                lax.broadcasted_iota(jnp.int32, shape, 1)
                == lax.broadcasted_iota(jnp.int32, shape, 0) * 8 + i,
                1.0,
                0.0,
            ).astype(BF)
            out_ref[:, i * lanes : (i + 1) * lanes] = nn(pick, block).astype(BF)


def expert_kernel(going, coming, gate, up, down, out_f, out_b, rows, acc):
    half = going.shape[0]
    features = gate.shape[1]
    step = pl.program_id(0)

    @pl.when(step == 0)
    def _():
        rows[:half, :] = going[...]
        rows[half:, :] = coming[...]
        acc[...] = jnp.zeros_like(acc)

    row_input = rows[:, :features]
    row_grad = rows[:, features:]
    gate_mat = gate[...]
    up_mat = up[...]
    gate_pre = nt(row_input, gate_mat)
    up_pre = nt(row_input, up_mat)
    hidden_grad = nt(row_grad, down[...])
    gate_sig = 1.0 / (1.0 + jnp.exp(-gate_pre))
    gate_grad = (hidden_grad * up_pre * gate_sig * (1.0 + gate_pre * (1.0 - gate_sig))).astype(BF)
    up_grad = (hidden_grad * gate_pre * gate_sig).astype(BF)
    acc[...] += nn(gate_grad, gate_mat) + nn(up_grad, up_mat)

    @pl.when(step == pl.num_programs(0) - 1)
    def _():
        out_f[...] = acc[:half, :].astype(out_f.dtype)
        out_b[...] = acc[half:, :].astype(out_b.dtype)


def expert_step(going, coming, gate, up, down, keep):
    half, width = going.shape
    hidden, features = gate.shape
    block = hidden // 3
    spec = pl.BlockSpec((block, features), lambda i: (i, 0))
    return pl.pallas_call(
        expert_kernel,
        grid=(3,),
        in_specs=[whole((half, width))] * 2 + [spec] * 3,
        out_specs=[whole((half, features))] * 2,
        out_shape=[jax.ShapeDtypeStruct((half, features), keep)] * 2,
        scratch_shapes=[pltpu.VMEM((2 * half, width), BF), pltpu.VMEM((2 * half, features), F32)],
        compiler_params=pltpu.CompilerParams(vmem_limit_bytes=WIDE),
        name="expert_step",
    )(going, coming, gate, up, down)


def add_kernel(part_f, part_b, recv_f, recv_b, out_f, out_b):
    out_f[...] = (part_f[...] + recv_f[...].astype(F32)).astype(BF)
    out_b[...] = (part_b[...] + recv_b[...].astype(F32)).astype(BF)


def heads_kernel(at_ref, *refs):
    rows = refs[:Y_COUNT]
    weights = refs[Y_COUNT : Y_COUNT + GROUP]
    out_ref = refs[Y_COUNT + GROUP]
    tokens = rows[0].shape[0]
    stack = jnp.concatenate([row[...].astype(F32) for row in rows], 0).astype(BF)
    y_at, x_at, core = at_ref[0], at_ref[1], at_ref[2]
    for shift in range(X_COUNT):
        for other in range(2):
            product = nt(stack, weights[2 * shift + other][...])
            to = ((x_at + shift) & (X_COUNT - 1)) * 2 + (core + other - 2 * core * other)
            for row in range(Y_COUNT):
                out_ref[to, (y_at + row) & (Y_COUNT - 1)] = product[
                    row * tokens : (row + 1) * tokens, :
                ].astype(BF)


def finish_kernel(own_f, own_b, recv_f, recv_b, out_ref):
    lanes = out_ref.shape[1]
    sums = jnp.concatenate(
        [own_f[...] + recv_f[...].astype(F32), own_b[...] + recv_b[...].astype(F32)], 0
    )
    count, features = sums.shape
    pieces = features // lanes
    stack = jnp.concatenate(
        [sums[:, i * lanes : (i + 1) * lanes] for i in range(pieces)], 0
    ).astype(BF)
    shape = (count * pieces, count * pieces)
    row = lax.broadcasted_iota(jnp.int32, shape, 0)
    column = lax.broadcasted_iota(jnp.int32, shape, 1)
    pick = jnp.where(column == (row & (pieces - 1)) * count + (row >> 2), 1.0, 0.0).astype(BF)
    out_ref[...] = nn(pick, stack).astype(BF)


def resid_kernel(returned_ref, residual_ref, gain_ref, grad_ref, experts_ref, out_ref):
    tokens, features = residual_ref.shape
    lanes = returned_ref.shape[1]
    pieces = features // lanes
    place0, place1 = slot_places(experts_ref[...], EXPERTS)
    at0 = as_column(place0).astype(jnp.int32) * pieces
    at1 = as_column(place1).astype(jnp.int32) * pieces
    returned = returned_ref[...]
    shape = (tokens, returned.shape[0])
    column = lax.broadcasted_iota(jnp.int32, shape, 1)
    moe = []
    for i in range(pieces):
        pick = jnp.where(column == at0 + i, 1.0, 0.0) + jnp.where(column == at1 + i, 1.0, 0.0)
        moe.append(nn(pick.astype(BF), returned))
    scaled = gain_ref[...] * jnp.concatenate(moe, 1)
    residual_f = residual_ref[...].astype(F32)
    factor = unit_scale(residual_f)
    unit_rows = residual_f * factor
    inner = jnp.mean(unit_rows * scaled, axis=-1, keepdims=True)
    total = grad_ref[...].astype(F32) + factor * (scaled - unit_rows * inner)
    out_ref[...] = total.astype(BF)


def single(kernel, shapes, *operands, grant=40 << 20):
    return pl.pallas_call(
        kernel,
        out_shape=[jax.ShapeDtypeStruct(shape, BF) for shape in shapes],
        compiler_params=pltpu.CompilerParams(vmem_limit_bytes=grant),
    )(*operands)


def body(
    query_rows,
    key_rows,
    value_rows,
    log_decay,
    residual,
    norm_gain,
    out_grad,
    experts_of,
    route_weight,
    output_weight,
    expert_gate,
    expert_up,
    expert_down,
):
    ctx_count = lax.axis_size("ctx")
    exp_count = lax.axis_size("exp")
    token_count, features = residual.shape
    block_len, head_size = query_rows.shape
    score_scale = 1.0 / math.sqrt(head_size * block_len * ctx_count)
    forward = [(i, (i + 1) % ctx_count) for i in range(ctx_count)]
    backward = [(i, (i - 1) % ctx_count) for i in range(ctx_count)]

    gain_row = norm_gain.reshape(1, features)
    experts = jnp.swapaxes(experts_of, 0, 1)
    (outgoing,) = single(
        pack_kernel,
        [(exp_count * 16, features // 4)],
        residual,
        gain_row,
        out_grad,
        experts,
        jnp.swapaxes(route_weight, 0, 1),
        grant=59 << 20,
    )
    arrived = lax.all_to_all(outgoing, "exp", split_axis=0, concat_axis=0, tiled=True)

    place = lax.axis_index("exp")
    core = place % 2
    x_at = (place // 2) % X_COUNT
    y_at = place // GROUP
    near = []
    for shift in range(X_COUNT):
        for other in range(2):
            if shift or other:
                link = [
                    (i, (i // 8) * 8 + ((i // 2 - shift) % X_COUNT) * 2 + (i % 2 ^ other))
                    for i in range(exp_count)
                ]
                near.append(lax.ppermute(output_weight, "exp", link))
            else:
                near.append(output_weight)

    levels = jnp.cumsum(log_decay[0])
    block_total = levels[-1]
    from_start = jnp.exp(levels)
    to_end = jnp.exp(block_total - levels)
    key_state = tn((key_rows.astype(F32) * to_end[:, None]).astype(BF), value_rows)
    gate_t = jnp.swapaxes(expert_gate[0], 0, 1)
    up_t = jnp.swapaxes(expert_up[0], 0, 1)
    down = expert_down[0]
    going, coming = single(unpack_kernel, [(exp_count, 2 * features)] * 2, arrived)
    sums = None
    for step in range(ctx_count):
        if step < ctx_count - 1:
            next_going = lax.ppermute(going, "ctx", forward)
            next_coming = lax.ppermute(coming, "ctx", backward)
        part = expert_step(going, coming, gate_t, up_t, down, BF if step == 1 else F32)
        if step == 0:
            own = part
        else:
            if step > 1:
                part = single(add_kernel, [part[0].shape] * 2, *part, *sums)
            sum_f = lax.ppermute(part[0], "ctx", forward)
            sum_b = lax.ppermute(part[1], "ctx", backward)
            sums = (sum_f, sum_b)
        going, coming = next_going, next_coming
    (summed,) = single(finish_kernel, [(exp_count * 8, features // 4)], *own, *sums)

    returned = lax.all_to_all(summed, "exp", split_axis=0, concat_axis=0, tiled=True)
    (resid_grad,) = single(
        resid_kernel,
        [(token_count, features)],
        returned,
        residual,
        gain_row,
        out_grad,
        experts,
        grant=59 << 20,
    )

    lines = [[j * GROUP + i for i in range(GROUP)] for j in range(Y_COUNT)]
    around = [resid_grad]
    for shift in range(1, Y_COUNT):
        link = [(i, (i - shift * GROUP) % exp_count) for i in range(exp_count)]
        around.append(lax.ppermute(resid_grad, "exp", link))
    spot = jnp.stack([y_at, x_at, core]).astype(jnp.int32)
    attn_part = pl.pallas_call(
        heads_kernel,
        in_specs=[pl.BlockSpec(memory_space=pltpu.SMEM)]
        + [pl.BlockSpec(memory_space=pltpu.VMEM)] * (Y_COUNT + GROUP),
        out_shape=jax.ShapeDtypeStruct((GROUP, Y_COUNT, token_count, head_size), BF),
        compiler_params=pltpu.CompilerParams(vmem_limit_bytes=40 << 20),
        name="head_rows",
    )(spot, *around, *near)
    attn_grad = lax.all_to_all(
        attn_part, "exp", split_axis=0, concat_axis=0, tiled=True, axis_index_groups=lines
    )
    attn_grad = jnp.transpose(attn_grad, (1, 0, 2, 3)).reshape(block_len, head_size)

    adjoint = score_scale * tn((query_rows.astype(F32) * from_start[:, None]).astype(BF), attn_grad)
    here = lax.axis_index("ctx")
    order8 = jnp.arange(ctx_count, dtype=jnp.int32)
    outward = jnp.where((order8 > here)[:, None, None], key_state[None], adjoint[None]).astype(BF)
    top = lax.reduce_precision(block_total, 8, 7)
    middle = lax.reduce_precision(block_total - top, 8, 7)
    bottom = block_total - top - middle
    line = jnp.stack([top, middle, bottom] + [jnp.zeros((), F32)] * 5).astype(BF)
    line = jnp.broadcast_to(line[None, :, None], (ctx_count, 8, head_size))
    outward = jnp.concatenate([outward, line], 1)
    inward = lax.all_to_all(outward, "ctx", split_axis=0, concat_axis=0, tiled=True)
    totals = jnp.sum(inward[:, head_size : head_size + 3, 0].astype(F32), axis=1)
    between = (order8[None, :] > jnp.minimum(order8, here)[:, None]) & (
        order8[None, :] < jnp.maximum(order8, here)[:, None]
    )
    reach = jnp.exp(jnp.sum(jnp.where(between, totals[None, :], 0.0), axis=1))
    blocks = inward[:, :head_size, :].astype(F32)
    state_in = jnp.sum(jnp.where(order8 < here, reach, 0.0)[:, None, None] * blocks, axis=0)
    adjoint_out = jnp.sum(jnp.where(order8 > here, reach, 0.0)[:, None, None] * blocks, axis=0)

    order = jnp.arange(block_len, dtype=jnp.int32)
    causal = order[:, None] >= order[None, :]
    fading = jnp.exp(jnp.where(causal, levels[:, None] - levels[None, :], -jnp.inf))
    probs = (score_scale * nt(query_rows, key_rows) * fading).astype(BF)
    pull = (score_scale * nt(attn_grad, value_rows) * fading).astype(BF)
    query_out = nn(pull, key_rows) + score_scale * from_start[:, None] * nt(attn_grad, state_in.astype(BF))
    adjoint_bf = adjoint_out.astype(BF)
    key_out = tn(pull, query_rows) + to_end[:, None] * nt(value_rows, adjoint_bf)
    value_out = tn(probs, attn_grad) + to_end[:, None] * nn(key_rows, adjoint_bf)
    return query_out.astype(BF), key_out.astype(BF), value_out.astype(BF)


def solution(mesh):
    placed = (
        P("ctx", "exp"),
        P("ctx", "exp"),
        P("ctx", "exp"),
        P("exp", "ctx"),
        P(("ctx", "exp"), None),
        P(),
        P(("ctx", "exp"), None),
        P(("ctx", "exp"), None),
        P(("ctx", "exp"), None),
        P("exp", None),
        P("exp", None, "ctx"),
        P("exp", None, "ctx"),
        P("exp", "ctx", None),
    )
    return jax.shard_map(
        body,
        mesh=mesh,
        in_specs=placed,
        out_specs=(P("ctx", "exp"), P("ctx", "exp"), P("ctx", "exp")),
        check_vma=False,
    )
```
